32 devices in a mesh: inst: 2 (over core), lon: 16 (over z, y, x).
Axes of the slice: x: 2, y: 2, z: 4, core: 2. Of those that a mesh axis runs over, the one named last changes fastest.
Arguments:
- obs_x: bfloat16 [384, 128, 256], P(('inst', 'lon')), may hold values from -6 to 6
- obs_cot: bfloat16 [384, 128, 256], P(('inst', 'lon')), may hold values from -6 to 6
- tile_window: int32 [384, 2], P(('inst', 'lon')), may hold values from 0 to 179, as said below
- point_mask: int32 [384, 128], P(('inst', 'lon')), may hold values from 0 to 1, as said below
- band_counts: int32 [32], P(('inst', 'lon')), may hold values from 1 to 12, as said below
- latents: bfloat16 [64, 184, 256], P('lon'), may hold values from -6 to 6
- w_query: bfloat16 [256, 128], replicated, may hold values from -3 to 3
- w_key: bfloat16 [256, 128], replicated, may hold values from -0.375 to 0.375
- w_value: bfloat16 [256, 128], replicated, may hold values from -0.375 to 0.375
- w_out: bfloat16 [128, 256], replicated, may hold values from -0.5 to 0.5
Outputs:
- decoded: bfloat16 [384, 128, 256], P(('inst', 'lon'))
- obs_grad: bfloat16 [384, 128, 256], P(('inst', 'lon'))
- latent_grad: float32 [64, 184, 256], P('lon')
- query_grad: float32 [256, 128], replicated
- key_grad: float32 [256, 128], replicated
- value_grad: float32 [256, 128], replicated
- out_grad: float32 [128, 256], replicated
The draws below stay inside these ranges and needn't reach their ends.
Inputs may be any that keep to these rules, and one draw needn't show every extreme that they name: `tile_window`: column 0 is the first longitude column of the tile's window; the window's centre column (column 2) mod 64 is one of the 4 columns of the band that holds the tile. Column 1 is the window's first latitude row, at most 179. `point_mask`: in each tile the live slots come first, and half or more of the slots are live. `band_counts`: one entry equals 12.
All inputs are finite; a program needn't handle non-finite values.
Results may differ from the reference program's by a relative error of at most 0.007.
The reference program's roundings to bfloat16 on the way count: a program that leaves them out, or rounds other values in their place, can miss the bound.
Values may be sent and summed in bfloat16 or wider, within the bound.
A program may use at most 64 MiB of HBM per device.

```python
import math
import jax
import jax.numpy as jnp
from jax import lax

D = 256
HEADS = 4
ATTN = 128
TILE = 128
TILES_DEV = 12
LC_DEV = 4
NLAT = 184
REACH = 2
LONS = 64
TILES = 384
N_INST = 2
N_LON = 16


def draw_band_counts(key, part):
    devices_all = N_INST * N_LON
    first, second = jax.random.split(key)
    spread = jax.random.randint(first, (devices_all,), 0, TILES_DEV)
    counts = 1 + spread * spread // TILES_DEV
    fullest = jax.random.randint(second, (), 0, devices_all)
    return jnp.where(jnp.arange(devices_all) == fullest, TILES_DEV, counts).astype(jnp.int32)


def draw_point_mask(key, part):
    tile_total = TILES_DEV * N_INST * N_LON
    live_len = jax.random.randint(key, (tile_total, 1), TILE // 2, TILE + 1)
    return (jnp.arange(TILE)[None, :] < live_len).astype(jnp.int32)


def draw_tile_window(key, part):
    tile_total = TILES_DEV * N_INST * N_LON
    first, second = jax.random.split(jax.random.fold_in(key, 7))
    tile_ids = jnp.arange(tile_total)
    bands = tile_ids // TILES_DEV % N_LON
    offset = jax.random.randint(first, (tile_total,), 0, LC_DEV)
    offset = jnp.where(tile_ids == 0, REACH - 1, jnp.where(tile_ids == 1, REACH, offset))
    centre = bands * LC_DEV + offset
    column = (centre - REACH) % LONS
    lat_first = jax.random.randint(second, (tile_total,), 0, NLAT - 2 * REACH)
    lat_first = jnp.where(tile_ids == 0, NLAT - 2 * REACH - 1, jnp.where(tile_ids == 1, 0, lat_first))
    return jnp.stack([column, lat_first], axis=1).astype(jnp.int32)


def level_of(own_key, extent, cuts, least, top_value):
    level, own = 1.0, jax.random.fold_in(own_key, 6)
    for position, parts in cuts:
        draws = jnp.exp(jax.random.uniform(jax.random.fold_in(own, position), (parts,), jnp.float32, least / len(cuts), top_value / len(cuts)))
        level = level * jnp.repeat(draws, extent[position] // parts).reshape([-1 if axis == position else 1 for axis in range(len(extent))])
    return level


def centred(stream_key, shape, width, reach, cuts=(), kind=jnp.bfloat16):
    values = jax.random.normal(stream_key, shape, jnp.float32) * width
    if len(cuts) > 0:
        values = level_of(stream_key, shape, cuts, -0.22, 0.18) * values
    return jnp.clip(values, min=-reach, max=reach).astype(kind)


def setup_inputs(seed: int = 0) -> dict:
    streams_of = jax.random.split(jax.random.key(seed), 11)
    obs_x = centred(streams_of[0], (TILES, TILE, D), 1.0, 6.0, ((0, 32),))
    obs_cot = centred(streams_of[1], (TILES, TILE, D), 1.0, 6.0, ((0, 32),))
    tile_window = draw_tile_window(jax.random.fold_in(streams_of[10], 71), 0)
    point_mask = draw_point_mask(jax.random.fold_in(streams_of[10], 71), 0)
    band_counts = draw_band_counts(jax.random.fold_in(streams_of[10], 71), 0)
    latents = centred(streams_of[5], (LONS, NLAT, D), 1.0, 6.0, ((0, 16),))
    w_query = centred(streams_of[6], (D, ATTN), (D // 64) ** -0.5, 3.0)
    w_key = centred(streams_of[7], (D, ATTN), D ** -0.5, 0.375)
    w_value = centred(streams_of[8], (D, ATTN), D ** -0.5, 0.375)
    w_out = centred(streams_of[9], (ATTN, D), ATTN ** -0.5, 0.5)
    return {"obs_x": obs_x, "obs_cot": obs_cot, "tile_window": tile_window, "point_mask": point_mask, "band_counts": band_counts, "latents": latents, "w_query": w_query, "w_key": w_key, "w_value": w_value, "w_out": w_out}


softcap = 30.0

def split_products(grad, w_pair, flat_latents):
    grad_high = grad.astype(jnp.bfloat16)
    grad_low = (grad - grad_high.astype(jnp.float32)).astype(jnp.bfloat16)
    by_rows = (((1,), (1,)), ((), ()))
    by_cols = (((0,), (0,)), ((), ()))
    latent_part = lax.dot_general(grad_high, w_pair, by_rows, preferred_element_type=jnp.float32) + lax.dot_general(grad_low, w_pair, by_rows, preferred_element_type=jnp.float32)
    pair_weight = lax.dot_general(flat_latents, grad_high, by_cols, preferred_element_type=jnp.float32) + lax.dot_general(flat_latents, grad_low, by_cols, preferred_element_type=jnp.float32)
    return (latent_part, pair_weight)

def attend(obs_x, obs_cot, live_points, windows, w_query, w_out):
    n_tiles, tile_len, model_width = obs_x.shape
    attn_width = w_query.shape[1]
    head_size = attn_width // HEADS
    score_scale = 1.0 / math.sqrt(head_size)
    flat_x = obs_x.reshape(-1, model_width)
    queries = jnp.dot(flat_x, w_query, preferred_element_type=jnp.float32).astype(jnp.bfloat16)
    query_heads = queries.reshape(n_tiles, tile_len, HEADS, head_size)
    win_keys = windows[:, :, :attn_width].reshape(n_tiles, -1, HEADS, head_size)
    win_values = windows[:, :, attn_width:].reshape(n_tiles, -1, HEADS, head_size)
    raw_scores = jnp.einsum('nqhd,nkhd->nhqk', query_heads.astype(jnp.float32), win_keys.astype(jnp.float32)) * score_scale
    capped = softcap * jnp.tanh(raw_scores / softcap)
    weights = jnp.exp(capped)
    probs = weights / lax.optimization_barrier(jnp.sum(weights, axis=-1, keepdims=True))
    probs_b = probs.astype(jnp.bfloat16)
    attended = jnp.einsum('nhqk,nkhd->nqhd', probs_b.astype(jnp.float32), win_values.astype(jnp.float32))
    attended = attended.astype(jnp.bfloat16).reshape(-1, attn_width)
    projected = jnp.dot(attended, w_out, preferred_element_type=jnp.float32).reshape(n_tiles, tile_len, model_width)
    decoded = (obs_x.astype(jnp.float32) + live_points[:, :, None] * projected).astype(jnp.bfloat16)
    masked = obs_cot * live_points.astype(jnp.bfloat16)[:, :, None]
    flat_cot = masked.reshape(-1, model_width)
    out_grad = jnp.dot(attended.T, flat_cot, preferred_element_type=jnp.float32)
    attended_grad = jnp.dot(flat_cot, w_out.T, preferred_element_type=jnp.float32).astype(jnp.bfloat16)
    attended_grad = attended_grad.reshape(n_tiles, tile_len, HEADS, head_size)
    prob_grad = jnp.einsum('nqhd,nkhd->nhqk', attended_grad.astype(jnp.float32), win_values.astype(jnp.float32))
    row_inner = lax.optimization_barrier(jnp.sum(probs * prob_grad, axis=-1, keepdims=True))
    score_grad = (probs * (prob_grad - row_inner) * (1.0 - (capped / softcap) ** 2) * score_scale).astype(jnp.bfloat16)
    query_part = jnp.einsum('nhqk,nkhd->nqhd', score_grad.astype(jnp.float32), win_keys.astype(jnp.float32))
    query_part = query_part.astype(jnp.bfloat16).reshape(-1, attn_width)
    key_part = jnp.einsum('nhqk,nqhd->nkhd', score_grad.astype(jnp.float32), query_heads.astype(jnp.float32))
    value_part = jnp.einsum('nhqk,nqhd->nkhd', probs_b.astype(jnp.float32), attended_grad.astype(jnp.float32))
    window_grad = jnp.concatenate([key_part.reshape(n_tiles, -1, attn_width), value_part.reshape(n_tiles, -1, attn_width)], axis=-1)
    obs_grad = obs_cot.astype(jnp.float32).reshape(-1, model_width) + jnp.dot(query_part, w_query.T, preferred_element_type=jnp.float32)
    obs_grad = obs_grad.astype(jnp.bfloat16).reshape(n_tiles, tile_len, model_width)
    query_grad = jnp.dot(flat_x.T, query_part, preferred_element_type=jnp.float32)
    return (decoded, obs_grad, window_grad, query_grad, out_grad)

def reference(obs_x, obs_cot, tile_window, point_mask, band_counts, latents, w_query, w_key, w_value, w_out):
    lon_cols, lat_rows, model_width = latents.shape
    attn_width = w_query.shape[1]
    window = 2 * REACH + 1
    w_pair = jnp.concatenate([w_key, w_value], axis=1)
    flat_latents = latents.reshape(-1, model_width)
    pairs = jnp.dot(flat_latents, w_pair, preferred_element_type=jnp.float32).astype(jnp.bfloat16)
    offsets = jnp.arange(window, dtype=jnp.int32)
    columns = (tile_window[:, 0:1] + offsets[None, :]) % lon_cols
    lat_index = tile_window[:, 1:2] + offsets[None, :]
    key_index = (columns[:, :, None] * lat_rows + lat_index[:, None, :]).reshape(-1, window * window).astype(jnp.int32)
    tile_total, tile_len = point_mask.shape
    device_total = tile_total // TILES_DEV
    local_tile = jnp.arange(tile_total, dtype=jnp.int32) % TILES_DEV
    counts = jnp.repeat(band_counts, TILES_DEV, total_repeat_length=tile_total)
    live_points = point_mask.astype(jnp.float32) * (local_tile < counts).astype(jnp.float32)[:, None]

    def per_device(device_block):
        block_x, block_cot, block_live, block_index = device_block
        windows = jnp.take(pairs, block_index, axis=0)
        return attend(block_x, block_cot, block_live, windows, w_query, w_out)
    results = lax.map(per_device, (obs_x.reshape(device_total, TILES_DEV, tile_len, model_width), obs_cot.reshape(device_total, TILES_DEV, tile_len, model_width), live_points.reshape(device_total, TILES_DEV, tile_len), key_index.reshape(device_total, TILES_DEV, window * window)))
    decoded = results[0].reshape(obs_x.shape)
    obs_grad = results[1].reshape(obs_x.shape)
    window_grad = results[2].reshape(-1, 2 * attn_width)
    query_grad = lax.optimization_barrier(jnp.sum(results[3], axis=0))
    out_grad = lax.optimization_barrier(jnp.sum(results[4], axis=0))
    pair_grad = jnp.zeros((lon_cols * lat_rows, 2 * attn_width), jnp.float32).at[key_index.reshape(-1)].add(window_grad)
    latent_grad, pair_weight = split_products(pair_grad, w_pair, flat_latents)
    return (decoded, obs_grad, latent_grad.reshape(lon_cols, lat_rows, model_width), query_grad, pair_weight[:, :attn_width], pair_weight[:, attn_width:], out_grad)
```

```python
import functools
import math

import jax
import jax.numpy as jnp
from jax import lax
from jax.experimental import pallas as pl
from jax.experimental.pallas import tpu as pltpu
from jax.sharding import PartitionSpec as P

HEADS = 4
REACH = 2
WINDOW = 2 * REACH + 1
SUB = 8
CAP = 30.0
MESH = pl.DeviceIdType.MESH
F32 = jnp.float32
BF16 = jnp.bfloat16

NT = (((1,), (1,)), ((), ()))
TN = (((0,), (0,)), ((), ()))


def dot(a, b, dims=(((1,), (0,)), ((), ()))):
    return lax.dot_general(a, b, dims, preferred_element_type=F32)


def send(src, dst, send_sem, recv_sem, target):
    copy = pltpu.make_async_remote_copy(
        src_ref=src, dst_ref=dst, send_sem=send_sem, recv_sem=recv_sem, device_id=target,
        device_id_type=MESH)
    copy.start()
    return copy


def fused_kernel(
    n_inst, n_lon, parts, gp, lat_rows, band_cols,
    tw_hbm, cnt_hbm, x_hbm, cot_hbm, mask_hbm, lat_hbm, wq_hbm, wk_hbm, wv_hbm, wo_hbm,
    dec, og, lat_out, q_out, k_out, v_out, o_out,
    tw, cnt, x, cot, mask, lat, wq, wp, wo, near, wide_a, wide_b, queries, attg, masked, x_t, m_t,
    lat_win, pair_win, kv, att, qp, own, halo, g, own_in, pre, hsum, hbuf, hall,
    rs, part, mine, gpre, gsum, ag,
    load, halo_s, halo_r, fan_s, fan_r, b_s, b_r, h_s, h_r, j_s, j_r, i_s, i_r,
    rs_s, rs_r, p_s, p_r, a_s, a_r, f_s, f_r, local,
):
    me, mi = lax.axis_index("lon"), lax.axis_index("inst")
    slot = mi if parts > 1 else 0
    tiles, length, width = x.shape
    attn = wq.shape[1]
    head = attn // HEADS
    scale = 1.0 / math.sqrt(head)
    own_rows, half = lat_rows * band_cols, near.shape[2]
    edge = parts * half
    total_rows = own_rows + 2 * edge
    slots = WINDOW * SUB
    lon_cols = band_cols * n_lon

    def lon_at(d):
        return lax.rem(me + d, n_lon)

    def inst_at(d):
        return lax.rem(mi + d, n_inst)

    bits = [b for b in range(n_lon.bit_length() - 1)]

    def pair(k):
        if n_lon != 2 ** len(bits):
            return lon_at(k)
        return me + sum(2 ** b * (1 - 2 * lax.rem(me // 2 ** b, 2)) for b in bits if k >> b & 1)

    def back(k):
        return pair(k if n_lon == 2 ** len(bits) else n_lon - k)

    far_first = sorted(range(1, n_lon), key=lambda k: -((k & 1) + (k >> 1 & 1) + (k >> 2)))

    barrier = pltpu.get_barrier_semaphore()
    for d in range(1, n_lon):
        pl.semaphore_signal(barrier, inc=1, device_id={"lon": lon_at(d)}, device_id_type=MESH)
    for d in range(1, n_inst):
        pl.semaphore_signal(barrier, inc=1, device_id={"inst": inst_at(d)}, device_id_type=MESH)
    loads = [
        pltpu.make_async_copy(src, dst, load.at[k])
        for k, (src, dst) in enumerate((
            (lat_hbm, lat), (x_hbm, x), (cot_hbm, cot), (mask_hbm, mask), (wq_hbm, wq),
            (wk_hbm, wp.at[:, pl.ds(0, attn)]), (wv_hbm, wp.at[:, pl.ds(attn, attn)]), (wo_hbm, wo),
            (tw_hbm, tw), (cnt_hbm, cnt)))
    ]
    for copy in loads:
        copy.start()
    pl.semaphore_wait(barrier, n_lon + n_inst - 2)

    peers = [inst_at(d) for d in range(1, n_inst)] if parts > 1 else []
    odd = lax.rem(me, 2)
    first = send(
        lat_hbm.at[parts * odd + slot], near.at[1 - odd, slot], halo_s.at[1 - odd],
        halo_r.at[1 - odd], {"lon": lon_at(n_lon - 1 + 2 * odd)})
    second = send(
        lat_hbm.at[parts * (1 - odd) + slot], near.at[odd, slot], halo_s.at[odd],
        halo_r.at[odd], {"lon": lon_at(1 + (n_lon - 2) * odd)})

    for copy in loads:
        copy.wait()

    wides = ((wide_a, pl.ds(0, width // 2)), (wide_b, pl.ds(width // 2, width // 2)))
    for ref, lanes in wides:
        ref[pl.ds(edge, own_rows), :] = lat[:, :, lanes].reshape(own_rows, width // 2).astype(F32)
        ref[pl.ds(total_rows, SUB), :] = jnp.zeros((SUB, width // 2), F32)
    row_id = lax.broadcasted_iota(jnp.int32, (length, width), 0)

    def prepare(t, carry):
        flat_x, flat_cot = x[t], cot[t]
        used = jnp.sum(mask[pl.ds(t, 1), :], axis=1, keepdims=True)
        used = jnp.where(t < cnt[0], used, 0)
        m = jnp.where(row_id < used, flat_cot.astype(F32), 0.0).astype(BF16)
        rows = pl.ds(pl.multiple_of(t * length, length), length)
        queries[rows, :] = dot(flat_x, wq[...]).astype(BF16)
        masked[rows, :] = m
        attg[rows, :] = dot(m, wo[...], NT).astype(BF16)
        x_t[:, rows] = flat_x.T
        m_t[:, rows] = m.T
        return carry

    lax.fori_loop(0, tiles, prepare, 0)

    fans = []
    for copy, side in ((first, 1 - odd), (second, odd)):
        copy.wait_recv()
        for d, other in enumerate(peers):
            fans.append(send(
                near.at[side, slot], near.at[side, slot], fan_s.at[side, d], fan_r.at[side, d],
                {"inst": other}))
    first.wait_send()
    second.wait_send()
    for copy in fans:
        copy.wait()
    for ref, lanes in wides:
        ref[pl.ds(0, edge), :] = near[0, :, :, lanes].reshape(edge, width // 2).astype(F32)
        ref[pl.ds(edge + own_rows, edge), :] = near[1, :, :, lanes].reshape(edge, width // 2).astype(F32)

    band_first = me * band_cols
    bases = []
    for t in range(tiles):
        col = lax.rem(tw[0, t] - band_first + REACH + lon_cols, lon_cols)
        base = jnp.minimum(col, band_cols - 1) * lat_rows + tw[1, t]
        bases.append(base)
        for ref, lanes in wides:
            lat_win[pl.ds(t * slots, slots), lanes] = jnp.concatenate(
                [ref[pl.ds(base + a * lat_rows, SUB), :] for a in range(WINDOW)], axis=0).astype(BF16)
    pair_win[...] = dot(lat_win[...], wp[...]).astype(BF16)

    lane = lax.broadcasted_iota(jnp.int32, (1, attn), 1) // head
    head_mask = [(lane == h).astype(F32) for h in range(HEADS)]
    slot_id = lax.broadcasted_iota(jnp.int32, (slots, length), 0)
    valid = ((slot_id & (SUB - 1)) < WINDOW)[None]

    def score(t):
        q_t, g_t = queries[pl.ds(t * length, length), :], attg[pl.ds(t * length, length), :]
        pw = pair_win[pl.ds(t * slots, slots), :].astype(F32)
        kw, vw = pw[:, :attn], pw[:, attn:]
        kb = jnp.concatenate([kw * m for m in head_mask], axis=0).astype(BF16)
        vb = jnp.concatenate([vw * m for m in head_mask], axis=0).astype(BF16)
        return q_t, g_t, kb, vb, dot(kb, q_t, NT), dot(vb, g_t, NT)

    def weigh(q_t, g_t, kb, vb, raw, dp):
        th = jnp.tanh(raw * (scale / CAP)).reshape(HEADS, slots, length)
        e = jnp.where(valid, jnp.exp(CAP * th), 0.0)
        p = e * (1.0 / jnp.sum(e, axis=1, keepdims=True))
        dp = dp.reshape(HEADS, slots, length)
        inner = jnp.sum(p * dp, axis=1, keepdims=True)
        sg = p * (dp - inner) * (scale - scale * th * th)
        sg = sg.reshape(HEADS * slots, length).astype(BF16)
        pb = p.reshape(HEADS * slots, length).astype(BF16)
        return q_t, g_t, kb, vb, pb, sg

    def gather_up(t, q_t, g_t, kb, vb, pb, sg):
        rows = pl.ds(t * length, length)
        att[rows, :] = dot(pb, vb, TN).astype(BF16)
        qp[rows, :] = dot(sg, kb, TN).astype(BF16)
        kp = dot(sg, q_t)
        vp = dot(pb, g_t)
        k_sum = sum(kp[h * slots : (h + 1) * slots] * head_mask[h] for h in range(HEADS))
        v_sum = sum(vp[h * slots : (h + 1) * slots] * head_mask[h] for h in range(HEADS))
        kv[pl.ds(t * slots, slots), :] = jnp.concatenate([k_sum, v_sum], axis=1)

    scored, weighed = score(0), None
    for t in range(tiles):
        ahead = score(t + 1) if t + 1 < tiles else None
        if weighed is not None:
            gather_up(t - 1, *weighed)
        weighed, scored = weigh(*scored), ahead
    gather_up(tiles - 1, *weighed)

    kv_all = kv[...]
    kv_high = kv_all.astype(BF16)
    kv_low = (kv_all - kv_high.astype(F32)).astype(BF16)
    w_grad = dot(lat_win[...], kv_high, TN) + dot(lat_win[...], kv_low, TN)
    rows = g.shape[1]
    at = 0
    for piece in (
        dot(x_t[...], qp[...]), w_grad[:, :attn], w_grad[:, attn:], dot(m_t[...], att[...]),
    ):
        count = piece.shape[0] // rows
        g[pl.ds(at, count)] = piece.astype(BF16).reshape(count, rows, attn)
        at += count

    presums = []
    if gp > 1:
        presums = [
            send(g.at[pl.ds(inst_at(d) * n_lon, n_lon)], gpre.at[d], p_s.at[d], p_r.at[d],
                 {"inst": inst_at(d)})
            for d in range(1, n_inst)
        ]

    lane_slot = lax.broadcasted_iota(jnp.int32, (1, tiles * slots), 1)
    target = jnp.zeros((1, tiles * slots), jnp.int32)
    for t in range(tiles):
        off = lane_slot - t * slots
        inside = (off >= 0) & (off < slots)
        target = jnp.where(
            inside, bases[t] + (off // SUB) * lat_rows + (off & (SUB - 1)), target)
    def scatter(picked):
        return dot(jnp.where(picked == target, 1.0, 0.0).astype(BF16), kv_high).astype(BF16)

    row_iota = lax.broadcasted_iota(jnp.int32, (2 * edge, tiles * slots), 0)
    row_iota = jnp.where(row_iota < edge, row_iota, row_iota + own_rows)
    halo[...] = scatter(row_iota).reshape(halo.shape)
    joined = []
    if parts > 1:
        for side in range(2):
            for d in range(1, n_inst):
                joined.append(send(
                    halo.at[side * parts + inst_at(d)], pre.at[side, d], b_s.at[side, d],
                    b_r.at[side, d], {"inst": inst_at(d)}))

    if gp > 1:
        for copy in presums:
            copy.wait()
        total = g[pl.ds(mi * n_lon, n_lon)].astype(F32)
        for d in range(1, n_inst):
            total = total + gpre[d].astype(F32)
        gsum[...] = total.astype(BF16)
        source = gsum
    else:
        source = g
    scatters = [
        send(source.at[pair(d)], rs.at[d], rs_s.at[d], rs_r.at[d], {"lon": pair(d)})
        for d in far_first
    ]
    for copy in joined:
        copy.wait()
    halos = []
    for side in range(2):
        total = halo[side * parts + slot].astype(F32)
        if parts > 1:
            for e in range(1, n_inst):
                total = total + pre[side, e].astype(F32)
        hsum[side] = total.astype(BF16)
    for side in (odd, 1 - odd):
        halos.append(send(
            hsum.at[side], hbuf.at[side], h_s.at[side], h_r.at[side],
            {"lon": lon_at(n_lon - 1 + 2 * side)}))
    row_iota = lax.broadcasted_iota(jnp.int32, (own_rows, tiles * slots), 0) + edge
    own[...] = scatter(row_iota).reshape(own.shape)
    joins = [
        send(own, own_in.at[d], j_s.at[d], j_r.at[d], {"inst": inst_at(d)})
        for d in range(1, n_inst)
    ]

    def outputs(t, carry):
        rows = pl.ds(pl.multiple_of(t * length, length), length)
        live = jnp.sum(mask[pl.ds(t, 1), :], axis=1, keepdims=True)
        live = jnp.where(t < cnt[0], live, 0)
        change = jnp.where(row_id < live, dot(att[rows, :], wo[...]), 0.0)
        dec[t] = (x[t].astype(F32) + change).astype(BF16)
        og[t] = (cot[t].astype(F32) + dot(qp[rows, :], wq[...], NT)).astype(BF16)
        return carry

    lax.fori_loop(0, tiles, outputs, 0)

    for copy in scatters:
        copy.wait()
    total = source[me].astype(F32)
    for d in range(1, n_lon):
        total = total + rs[d].astype(F32)
    if gp == 1:
        part[mi] = total
        swaps = [
            send(part.at[mi], part.at[mi], p_s.at[d], p_r.at[d], {"inst": inst_at(d)})
            for d in range(1, n_inst)
        ]
        for copy in swaps:
            copy.wait()
        total = part[0]
        for i in range(1, n_inst):
            total = total + part[i]
    mine[...] = total.astype(BF16)
    base = mi * n_lon if gp > 1 else 0
    gathers = [
        send(mine, ag.at[base + me], a_s.at[d], a_r.at[d], {"lon": pair(d)})
        for d in far_first
    ]
    fans = []
    if gp > 1:
        fans = [
            send(mine, ag.at[base + me], f_s.at[d, 0], f_r.at[d, 0], {"inst": inst_at(d)})
            for d in range(1, n_inst)
        ]
    keep = pltpu.make_async_copy(mine, ag.at[base + me], local.at[0])
    keep.start()
    for copy in joins:
        copy.wait()
    for copy in halos:
        copy.wait()
    relays = []
    if parts > 1:
        for d in range(1, n_inst):
            relays.append(send(
                hbuf, hall.at[d], i_s.at[d], i_r.at[d], {"inst": inst_at(d)}))

    def column(k):
        grad = own[k].astype(F32)
        for d in range(1, n_inst):
            grad = grad + own_in[d, k].astype(F32)
        return grad

    def finish(k, grad):
        grad_high = grad.astype(BF16)
        grad_low = (grad - grad_high.astype(F32)).astype(BF16)
        lat_out[k] = dot(grad_high, wp[...], NT) + dot(grad_low, wp[...], NT)

    for copy in relays:
        copy.wait()
    for side, first_col in ((1, 0), (0, parts)):
        for d in range(n_inst if parts > 1 else 1):
            grad_in = hbuf[side] if d == 0 else hall[d, side]
            k = first_col + (inst_at(d) if parts > 1 else 0)
            finish(k, column(k) + grad_in.astype(F32))

    for e, copy in reversed(list(zip(far_first, gathers))):
        copy.wait_recv()
        if gp > 1:
            at = base + back(e)
            for d in range(1, n_inst):
                fans.append(send(
                    ag.at[at], ag.at[at], f_s.at[d, e], f_r.at[d, e], {"inst": inst_at(d)}))
    for copy in gathers:
        copy.wait_send()
    for copy in fans + [keep]:
        copy.wait()
    at = 0
    for out in (q_out, k_out, v_out, o_out):
        count = width // rows
        piece = ag[pl.ds(at, count)].astype(F32).reshape(width, attn)
        out[...] = piece.T if out is o_out else piece
        at += count


def flush_kernel(*refs):
    count = (len(refs) - 1) // 2
    copies = [
        pltpu.make_async_copy(refs[k], refs[count + k], refs[-1].at[k]) for k in range(count)
    ]
    for copy in copies:
        copy.start()
    for copy in copies:
        copy.wait()


def shards(
    n_inst, n_lon, obs_x, obs_cot, tile_window, point_mask, band_counts, latents,
    w_query, w_key, w_value, w_out,
):
    n_tiles, length, width = obs_x.shape
    band_cols, lat_rows, _ = latents.shape
    attn = w_query.shape[1]
    edge, own_rows = REACH * lat_rows, band_cols * lat_rows
    wide = own_rows + 2 * edge
    parts = n_inst if edge % (SUB * n_inst) == 0 else 1
    half = edge // parts
    slots = WINDOW * SUB
    points = n_tiles * length
    dma = pltpu.SemaphoreType.DMA
    anywhere = pl.BlockSpec(memory_space=pl.ANY)
    in_vmem = pl.BlockSpec(memory_space=pltpu.VMEM)
    weight_rows = 4 * width
    rows = weight_rows // n_lon
    gp = n_inst if rows % (2 * SUB * n_inst) == 0 else 1
    rows = rows // gp
    vmem = pltpu.VMEM
    shapes = [
        (obs_x.shape, BF16), (obs_x.shape, BF16), ((2 * parts, half, width), F32),
        ((width, attn), F32), ((width, attn), F32), ((width, attn), F32), ((attn, width), F32),
    ]
    results = pl.pallas_call(
        functools.partial(fused_kernel, n_inst, n_lon, parts, gp, lat_rows, band_cols),
        out_shape=[vmem(s, t) for s, t in shapes],
        in_specs=[anywhere] * 10,
        out_specs=[in_vmem] * len(shapes),
        scratch_shapes=[
            pltpu.SMEM(tile_window.shape[::-1], jnp.int32), pltpu.SMEM((1,), jnp.int32),
            vmem(obs_x.shape, BF16), vmem(obs_x.shape, BF16), vmem((n_tiles, length), jnp.int32),
            vmem((2 * parts, half, width), BF16), vmem((width, attn), BF16),
            vmem((width, 2 * attn), BF16), vmem((attn, width), BF16),
            vmem((2, parts, half, width), BF16),
            vmem((wide + SUB, width // 2), F32), vmem((wide + SUB, width // 2), F32),
            vmem((points, attn), BF16), vmem((points, attn), BF16), vmem((points, width), BF16),
            vmem((width, points), BF16), vmem((width, points), BF16),
            vmem((n_tiles * slots, width), BF16), vmem((n_tiles * slots, 2 * attn), BF16),
            vmem((n_tiles * slots, 2 * attn), F32),
            vmem((points, attn), BF16), vmem((points, attn), BF16),
            vmem((2 * parts, half, 2 * attn), BF16), vmem((2 * parts, half, 2 * attn), BF16),
            vmem((gp * n_lon, rows, attn), BF16),
            vmem((n_inst, 2 * parts, half, 2 * attn), BF16),
            vmem((2, n_inst, half, 2 * attn), BF16),
            vmem((2, half, 2 * attn), BF16), vmem((2, half, 2 * attn), BF16),
            vmem((n_inst, 2, half, 2 * attn), BF16),
            vmem((n_lon, rows, attn), BF16), vmem((n_inst, rows, attn), F32),
            vmem((rows, attn), BF16), vmem((n_inst, n_lon, rows, attn), BF16),
            vmem((n_lon, rows, attn), BF16), vmem((gp * n_lon, rows, attn), BF16),
            dma((10,)), dma((2,)), dma((2,)), dma((2, n_inst)), dma((2, n_inst)),
            dma((2, n_inst)), dma((2, n_inst)), dma((2,)), dma((2,)),
            dma((n_inst,)), dma((n_inst,)), dma((n_inst,)), dma((n_inst,)),
            dma((n_lon,)), dma((n_lon,)), dma((n_inst,)), dma((n_inst,)),
            dma((n_lon,)), dma((n_lon,)), dma((n_inst, n_lon)), dma((n_inst, n_lon)), dma((1,)),
        ],
        compiler_params=pltpu.CompilerParams(collective_id=0, has_side_effects=True),
        name="fused",
    )(tile_window.T, band_counts, obs_x, obs_cot, point_mask,
      latents.reshape(2 * parts, half, width), w_query, w_key, w_value, w_out)
    results = [pltpu.with_memory_space_constraint(r, pltpu.VMEM) for r in results]
    decoded, obs_grad, latent_grad, query_grad, key_grad, value_grad, out_grad = pl.pallas_call(
        flush_kernel,
        out_shape=[jax.ShapeDtypeStruct(s, t) for s, t in shapes],
        in_specs=[in_vmem] * len(shapes),
        out_specs=[anywhere] * len(shapes),
        scratch_shapes=[dma((len(shapes),))],
        name="flush",
    )(*results)
    return (
        decoded,
        obs_grad,
        latent_grad.reshape(band_cols, lat_rows, width),
        query_grad,
        key_grad,
        value_grad,
        out_grad,
    )


def solution(mesh):
    placed = (
        P(("inst", "lon"), None, None),
        P(("inst", "lon"), None, None),
        P(("inst", "lon"), None),
        P(("inst", "lon"), None),
        P(("inst", "lon")),
        P("lon", None, None),
        P(),
        P(),
        P(),
        P(),
    )
    return jax.shard_map(
        functools.partial(shards, mesh.shape["inst"], mesh.shape["lon"]),
        mesh=mesh,
        in_specs=placed,
        out_specs=(
            P(("inst", "lon"), None, None),
            P(("inst", "lon"), None, None),
            P("lon", None, None),
            P(),
            P(),
            P(),
            P(),
        ),
        check_vma=False,
    )
```
